32 devices in a mesh: section: 2 (over x), wide: 4 (over z), tensor: 4 (over y, core).
Axes of the slice: x: 2, y: 2, z: 4, core: 2. Of those that a mesh axis runs over, the one named last changes fastest.
Arguments:
- boundary: float32 [2, 2, 1024, 2048], P('section', None, ('wide', 'tensor')), may hold values from -6 to 6
- positions: int32 [2, 1024], P(None, 'wide'), may hold values from 0 to 255, as said below
- attn_gain: bfloat16 [2, 2048], P('section', 'wide'), may hold values from 0.5 to 1.5
- w_query: bfloat16 [2, 2048, 2048], P('section', 'wide', 'tensor'), may hold values from -0.125 to 0.125
- w_key: bfloat16 [2, 2048, 2048], P('section', 'wide', 'tensor'), may hold values from -0.125 to 0.125
- w_value: bfloat16 [2, 2048, 2048], P('section', 'wide', 'tensor'), may hold values from -0.125 to 0.125
- w_out: bfloat16 [2, 2048, 2048], P('section', 'tensor', 'wide'), may hold values from -0.375 to 0.375
- mlp_gain: bfloat16 [2, 2048], P('section', 'wide'), may hold values from 0.5 to 1.5
- w_gate: bfloat16 [2, 2048, 8192], P('section', 'wide', 'tensor'), may hold values from -0.125 to 0.125
- w_up: bfloat16 [2, 2048, 8192], P('section', 'wide', 'tensor'), may hold values from -0.125 to 0.125
- w_down: bfloat16 [2, 8192, 2048], P('section', 'tensor', 'wide'), may hold values from -0.0625 to 0.0625
Outputs:
- ends: float32 [2, 2, 1024, 2048], P('section', None, ('wide', 'tensor'))
- grad_attn_gain: float32 [2, 2048], P('section', 'wide')
- grad_query: float32 [2, 2048, 2048], P('section', 'wide', 'tensor')
- grad_key: float32 [2, 2048, 2048], P('section', 'wide', 'tensor')
- grad_value: float32 [2, 2048, 2048], P('section', 'wide', 'tensor')
- grad_out: float32 [2, 2048, 2048], P('section', 'tensor', 'wide')
- grad_mlp_gain: float32 [2, 2048], P('section', 'wide')
- grad_gate: float32 [2, 2048, 8192], P('section', 'wide', 'tensor')
- grad_up: float32 [2, 2048, 8192], P('section', 'wide', 'tensor')
- grad_down: float32 [2, 8192, 2048], P('section', 'tensor', 'wide')
The draws below stay inside these ranges and needn't reach their ends.
Inputs may be any that keep to these rules, and one draw needn't show every extreme that they name: Within each sequence of 256 tokens the positions count up by one from 0 and restart at 0 at up to three drawn points; the first sequence of the first micro-batch has no restart.
All inputs are finite; a program needn't handle non-finite values.
Results may differ from the reference program's by a relative error of at most 0.025.
Values may be sent and summed in bfloat16 or wider, within the bound.
No kernel may reach another device: no remote copies, remote signals or barrier semaphores. Data moves between devices by JAX's collectives and lax.ppermute only.
A program may use at most 320 MiB of HBM per device.

```python
import jax
import jax.numpy as jnp
from jax import lax

D = 2048
HD = 64
FF = 8192
LEN = 256
MICRO = 2
MB_TOK = 1024


def draw_positions(key, part):
    number_seqs = MICRO * MB_TOK // LEN
    cut_points = jax.random.randint(key, (number_seqs, 3), 1, LEN)
    leading = jnp.arange(number_seqs)[:, None] == 0
    cut_points = jnp.where(leading, LEN, cut_points)
    offsets = jnp.arange(LEN)
    doc_start = jnp.max(jnp.where(cut_points[:, :, None] <= offsets[None, None, :], cut_points[:, :, None], 0), axis=1)
    return (offsets[None, :] - doc_start).reshape(MICRO, MB_TOK).astype(jnp.int32)


def shard_levels(key, shape, split, smallest, largest):
    factor_of = 1.0
    for position, parts in split:
        draws = jax.random.uniform(jax.random.fold_in(jax.random.fold_in(key, 6), position), (parts,), jnp.float32, smallest / len(split), largest / len(split))
        factor_of = factor_of * jnp.repeat(jnp.exp(draws), shape[position] // parts).reshape((-1,) + (1,) * (len(shape) - 1 - position))
    return factor_of


def bell_draw(own_key, shape, scale, limit, pieces=(), kind=jnp.bfloat16):
    drawn = scale * jax.random.normal(own_key, shape, jnp.float32)
    if pieces:
        drawn = drawn * shard_levels(own_key, shape, pieces, -0.22, 0.18)
    return jnp.clip(drawn, -limit, limit).astype(kind)


def setup_inputs(seed: int = 0) -> dict:
    key_of = jax.random.split(jax.random.key(seed), 12)
    return {
        "boundary": bell_draw(key_of[0], (2, MICRO, MB_TOK, D), 1.0, 6.0, ((0, 2), (2, 16)), jnp.float32),
        "positions": draw_positions(jax.random.fold_in(key_of[11], 71), 0),
        "attn_gain": jnp.clip(1.0 + 0.1 * jax.random.normal(key_of[2], (2, D), jnp.float32), 0.5, 1.5).astype(jnp.bfloat16),
        "w_query": bell_draw(key_of[3], (2, D, D), D ** -0.5, 0.125, ((0, 2), (1, 4), (2, 4))),
        "w_key": bell_draw(key_of[4], (2, D, D), D ** -0.5, 0.125, ((0, 2), (1, 4), (2, 4))),
        "w_value": bell_draw(key_of[5], (2, D, D), D ** -0.5, 0.125, ((0, 2), (1, 4), (2, 4))),
        "w_out": bell_draw(key_of[6], (2, D, D), (D // 8) ** -0.5, 0.375, ((0, 2), (1, 4), (2, 4))),
        "mlp_gain": jnp.clip(1.0 + 0.1 * jax.random.normal(key_of[7], (2, D), jnp.float32), 0.5, 1.5).astype(jnp.bfloat16),
        "w_gate": bell_draw(key_of[8], (2, D, FF), D ** -0.5, 0.125, ((0, 2), (1, 4), (2, 4))),
        "w_up": bell_draw(key_of[9], (2, D, FF), D ** -0.5, 0.125, ((0, 2), (1, 4), (2, 4))),
        "w_down": bell_draw(key_of[10], (2, FF, D), FF ** -0.5, 0.0625, ((0, 2), (1, 4), (2, 4))),
    }


eps_norm = 1e-05
rope_base = 130000.0

def rotate_half(values):
    half_size = values.shape[-1] // 2
    return jnp.concatenate([-values[..., half_size:], values[..., :half_size]], axis=-1)

def rope_tables(position_row, head_dim):
    half_size = head_dim // 2
    exponent = 2.0 * jnp.arange(half_size).astype(jnp.float32) / head_dim
    frequency = jnp.power(jnp.float32(rope_base), -exponent)
    angles = position_row.astype(jnp.float32)[:, None] * frequency[None, :]
    angles = jnp.concatenate([angles, angles], axis=-1)
    return (jnp.cos(angles)[:, None, :], jnp.sin(angles)[:, None, :])

def norm_rows(hidden, gain_row):
    inverse = lax.rsqrt(lax.optimization_barrier(jnp.mean(hidden * hidden, axis=-1, keepdims=True)) + eps_norm)
    return (hidden * inverse * gain_row.astype(jnp.float32), inverse)

def norm_back(hidden, inverse, gain_row, d_normed):
    scaled = d_normed * gain_row.astype(jnp.float32)
    d_hidden = inverse * scaled - hidden * inverse ** 3 * lax.optimization_barrier(jnp.mean(scaled * hidden, axis=-1, keepdims=True))
    return (d_hidden, lax.optimization_barrier(jnp.sum(d_normed * hidden * inverse, axis=0)))

def to_blocks(matrix):
    rows_all = matrix.shape[0]
    return matrix.reshape(rows_all // LEN, LEN, matrix.shape[1] // HD, HD).astype(jnp.float32)

def causal_scores(q_blocks, k_blocks):
    length = q_blocks.shape[1]
    scores = jnp.einsum('sqhd,skhd->shqk', q_blocks, k_blocks) * HD ** (-0.5)
    causal = jnp.arange(length)[:, None] >= jnp.arange(length)[None, :]
    return jnp.where(causal, scores, -jnp.inf)

def attend(query_rows, key_rows, value_rows):
    scores = causal_scores(to_blocks(query_rows), to_blocks(key_rows))
    row_max = lax.optimization_barrier(jnp.max(scores, axis=-1, keepdims=True))
    log_total = row_max + jnp.log(lax.optimization_barrier(jnp.sum(jnp.exp(scores - row_max), axis=-1, keepdims=True)))
    probs_low = jnp.exp(scores - log_total).astype(jnp.bfloat16)
    mixed_out = jnp.einsum('shqk,skhd->sqhd', probs_low.astype(jnp.float32), to_blocks(value_rows))
    return (mixed_out.reshape(query_rows.shape).astype(jnp.bfloat16), log_total)

def apply_rope(raw_rows, cos_table, sin_table):
    rows_all = raw_rows.shape[0]
    shaped = raw_rows.reshape(rows_all, -1, HD)
    return (shaped * cos_table + rotate_half(shaped) * sin_table).reshape(rows_all, -1)

def unrope(grad_rows, cos_table, sin_table):
    rows_all = grad_rows.shape[0]
    shaped = grad_rows.reshape(rows_all, -1, HD)
    return (shaped * cos_table - rotate_half(shaped) * sin_table).reshape(rows_all, -1)

def layer_forward(hidden, cos_table, sin_table, params):
    attn_gain, w_query, w_key, w_value, w_out, mlp_gain, w_gate, w_up, w_down = params
    normed1, inverse1 = norm_rows(hidden, attn_gain)
    normed1 = normed1.astype(jnp.bfloat16)
    q_raw = jnp.dot(normed1, w_query, preferred_element_type=jnp.float32)
    k_raw = jnp.dot(normed1, w_key, preferred_element_type=jnp.float32)
    value_rows = jnp.dot(normed1, w_value, preferred_element_type=jnp.float32).astype(jnp.bfloat16)
    query_rows = apply_rope(q_raw, cos_table, sin_table).astype(jnp.bfloat16)
    key_rows = apply_rope(k_raw, cos_table, sin_table).astype(jnp.bfloat16)
    attn_o, log_total = attend(query_rows, key_rows, value_rows)
    mid_stream = hidden + jnp.dot(attn_o, w_out, preferred_element_type=jnp.float32)
    normed2, inverse2 = norm_rows(mid_stream, mlp_gain)
    normed2 = normed2.astype(jnp.bfloat16)
    gate_pre = jnp.dot(normed2, w_gate, preferred_element_type=jnp.float32)
    up_pre = jnp.dot(normed2, w_up, preferred_element_type=jnp.float32)
    hidden_mlp = (jax.nn.silu(gate_pre) * up_pre).astype(jnp.bfloat16)
    final_rows = mid_stream + jnp.dot(hidden_mlp, w_down, preferred_element_type=jnp.float32)
    kept_values = (hidden, inverse1, normed1, query_rows, key_rows, value_rows, log_total, attn_o, mid_stream, inverse2, normed2, gate_pre, up_pre, hidden_mlp)
    return (final_rows, kept_values)

def layer_backward(cotangent, kept_values, params, cos_table, sin_table):
    attn_gain, w_query, w_key, w_value, w_out, mlp_gain, w_gate, w_up, w_down = params
    hidden, inverse1, normed1, query_rows, key_rows, value_rows, log_total, attn_o, mid_stream, inverse2, normed2, gate_pre, up_pre, hidden_mlp = kept_values
    c_low = cotangent.astype(jnp.bfloat16)
    d_hid = jnp.dot(c_low, w_down.T, preferred_element_type=jnp.float32)
    grad_down = jnp.dot(hidden_mlp.T, c_low, preferred_element_type=jnp.float32)
    sigmoid_gate = jax.nn.sigmoid(gate_pre)
    d_gate = (d_hid * up_pre * sigmoid_gate * (1.0 + gate_pre * (1.0 - sigmoid_gate))).astype(jnp.bfloat16)
    d_up = (d_hid * gate_pre * sigmoid_gate).astype(jnp.bfloat16)
    d_normed2 = jnp.dot(d_gate, w_gate.T, preferred_element_type=jnp.float32) + jnp.dot(d_up, w_up.T, preferred_element_type=jnp.float32)
    grad_gate = jnp.dot(normed2.T, d_gate, preferred_element_type=jnp.float32)
    grad_up = jnp.dot(normed2.T, d_up, preferred_element_type=jnp.float32)
    d_mid, grad_mlp_gain = norm_back(mid_stream, inverse2, mlp_gain, d_normed2)
    d_mid = cotangent + d_mid
    mid_low = d_mid.astype(jnp.bfloat16)
    grad_out = jnp.dot(attn_o.T, mid_low, preferred_element_type=jnp.float32)
    d_attn = jnp.dot(mid_low, w_out.T, preferred_element_type=jnp.float32).astype(jnp.bfloat16)
    q_blocks = to_blocks(query_rows)
    k_blocks = to_blocks(key_rows)
    v_blocks = to_blocks(value_rows)
    d_blocks = to_blocks(d_attn)
    scores = causal_scores(q_blocks, k_blocks)
    attn_probs = jnp.exp(scores - log_total)
    probs_low = attn_probs.astype(jnp.bfloat16).astype(jnp.float32)
    d_values = jnp.einsum('shqk,sqhd->skhd', probs_low, d_blocks).reshape(value_rows.shape).astype(jnp.bfloat16)
    d_probs = jnp.einsum('sqhd,skhd->shqk', d_blocks, v_blocks)
    row_dot = lax.optimization_barrier(jnp.sum(attn_probs * d_probs, axis=-1, keepdims=True))
    d_scores = (attn_probs * (d_probs - row_dot) * HD ** (-0.5)).astype(jnp.bfloat16).astype(jnp.float32)
    d_qrot = jnp.einsum('shqk,skhd->sqhd', d_scores, k_blocks).reshape(query_rows.shape)
    d_krot = jnp.einsum('shqk,sqhd->skhd', d_scores, q_blocks).reshape(key_rows.shape)
    d_query = unrope(d_qrot, cos_table, sin_table).astype(jnp.bfloat16)
    d_keys = unrope(d_krot, cos_table, sin_table).astype(jnp.bfloat16)
    d_normed1 = jnp.dot(d_query, w_query.T, preferred_element_type=jnp.float32) + jnp.dot(d_keys, w_key.T, preferred_element_type=jnp.float32) + jnp.dot(d_values, w_value.T, preferred_element_type=jnp.float32)
    grad_query = jnp.dot(normed1.T, d_query, preferred_element_type=jnp.float32)
    grad_key = jnp.dot(normed1.T, d_keys, preferred_element_type=jnp.float32)
    grad_value = jnp.dot(normed1.T, d_values, preferred_element_type=jnp.float32)
    d_hidden, grad_attn_gain = norm_back(hidden, inverse1, attn_gain, d_normed1)
    grad_sums = (grad_attn_gain, grad_query, grad_key, grad_value, grad_out, grad_mlp_gain, grad_gate, grad_up, grad_down)
    return (d_mid + d_hidden, grad_sums)

def reference(boundary, positions, attn_gain, w_query, w_key, w_value, w_out, mlp_gain, w_gate, w_up, w_down):
    weight_list = (attn_gain, w_query, w_key, w_value, w_out, mlp_gain, w_gate, w_up, w_down)
    layers = [tuple((stacked_arg[layer_index] for stacked_arg in weight_list)) for layer_index in range(2)]
    totals = [None, None]
    outputs = []
    input_grads = []
    for micro_index in range(MICRO):
        cos_table, sin_table = rope_tables(positions[micro_index], HD)
        middle, kept_first = layer_forward(boundary[0, micro_index], cos_table, sin_table, layers[0])
        final_rows, kept_second = layer_forward(middle, cos_table, sin_table, layers[1])
        d_middle, second_grads = layer_backward(boundary[1, micro_index], kept_second, layers[1], cos_table, sin_table)
        d_input, first_grads = layer_backward(d_middle, kept_first, layers[0], cos_table, sin_table)
        outputs.append(final_rows)
        input_grads.append(d_input)
        for layer_index, fresh in ((0, first_grads), (1, second_grads)):
            if totals[layer_index] is None:
                totals[layer_index] = fresh
            else:
                totals[layer_index] = tuple((old_sum + new_term for old_sum, new_term in zip(totals[layer_index], fresh)))
    ends = jnp.stack([jnp.stack(input_grads), jnp.stack(outputs)])
    stacked = tuple((jnp.stack([totals[0][slot_index], totals[1][slot_index]]) for slot_index in range(9)))
    return (ends, stacked[0], stacked[1], stacked[2], stacked[3], stacked[4], stacked[5], stacked[6], stacked[7], stacked[8])
```

```python
import functools

import jax
import jax.numpy as jnp
from jax import lax
from jax.experimental import pallas as pl
from jax.experimental.pallas import tpu as pltpu
from jax.sharding import PartitionSpec as P

HD = 64
LEN = 256
eps_norm = 1e-05
rope_base = 130000.0
SCALE = HD ** (-0.5)
F32 = jnp.float32
BF16 = jnp.bfloat16
LANES = 128
CHUNK = 1024

NN = (((1,), (0,)), ((), ()))
NT = (((1,), (1,)), ((), ()))
TN = (((0,), (0,)), ((), ()))


def mm(a, b, dims=NN):
    return lax.dot_general(a, b, dims, preferred_element_type=F32)


def partner(block, bits):
    return lax.ppermute(block, "tensor", [(i, i ^ bits) for i in range(lax.axis_size("tensor"))])


def gather_rows(own):
    pair = jnp.concatenate([own, partner(own, 2)], axis=0)
    return jnp.concatenate([pair, partner(pair, 1)], axis=0)


def scatter_rows(keep, send):
    half = keep.shape[0] // 2
    got = partner(send, 1).astype(F32)
    summed = keep + got
    last = partner(summed[half:].astype(BF16), 2)
    return summed[:half], last


def cost(flops, nbytes, trans=0):
    return pl.CostEstimate(flops=int(flops), bytes_accessed=int(nbytes), transcendentals=int(trans))


def norm_kernel(count, *refs):
    terms, gain_ref, h_ref, n_ref = refs[:count], refs[count], refs[count + 1], refs[count + 2]
    hidden = terms[0][...].astype(F32)
    for term in terms[1:]:
        hidden = hidden + term[...].astype(F32)
    inverse = lax.rsqrt(jnp.mean(hidden * hidden, axis=-1, keepdims=True) + eps_norm)
    h_ref[...] = hidden
    n_ref[...] = (hidden * inverse * gain_ref[...]).astype(BF16)


def add_norm(terms, gain_row):
    rows, width = terms[0].shape
    return pl.pallas_call(
        functools.partial(norm_kernel, len(terms)),
        out_shape=(
            jax.ShapeDtypeStruct((rows, width), F32),
            jax.ShapeDtypeStruct((rows, width), BF16),
        ),
        cost_estimate=cost(8 * rows * width, 16 * rows * width),
        name="add_norm",
    )(*terms, gain_row)


def norm_back_kernel(a_ref, b_ref, h_ref, gain_ref, c_ref, dh_ref, db_ref, gg_ref):
    d_normed = a_ref[...] + b_ref[...].astype(F32)
    hidden = h_ref[...]
    inverse = lax.rsqrt(jnp.mean(hidden * hidden, axis=-1, keepdims=True) + eps_norm)
    scaled = d_normed * gain_ref[...]
    average = jnp.mean(scaled * hidden, axis=-1, keepdims=True)
    grad = c_ref[...] + inverse * scaled - hidden * (inverse * inverse * inverse * average)
    dh_ref[...] = grad
    db_ref[...] = grad.astype(BF16)
    gg_ref[...] = jnp.sum(d_normed * hidden * inverse, axis=0, keepdims=True)


def norm_back(first, second, hidden, gain_row, cotangent):
    rows, width = hidden.shape
    return pl.pallas_call(
        norm_back_kernel,
        out_shape=(
            jax.ShapeDtypeStruct((rows, width), F32),
            jax.ShapeDtypeStruct((rows, width), BF16),
            jax.ShapeDtypeStruct((1, width), F32),
        ),
        cost_estimate=cost(16 * rows * width, 22 * rows * width),
        name="norm_back",
    )(first, second, hidden, gain_row, cotangent)


def rotated(block):
    lane = lax.broadcasted_iota(jnp.int32, block.shape, 1)
    low = lane % HD < HD // 2
    return jnp.where(
        low,
        -pltpu.roll(block, LANES - HD // 2, 1),
        pltpu.roll(block, HD // 2, 1),
    )


def attn_fwd_kernel(
    steps, n_ref, w_ref, wo_ref, cos_ref, sin_ref, ic_ref, ir_ref,
    qkv_ref, lse_ref, o_ref, keep_ref, send_ref, acc,
):
    phase, step = pl.program_id(0), pl.program_id(1)
    rows = n_ref.shape[0]
    heads_w = o_ref.shape[1]

    @pl.when(phase == 0)
    def _():
        term = mm(n_ref[...], w_ref[0])

        @pl.when(step == 0)
        def _():
            acc[...] = term

        @pl.when(step > 0)
        def _():
            acc[...] += term

        @pl.when(step == steps - 1)
        def _():
            cos, sin = cos_ref[...], sin_ref[...]
            seen = ic_ref[...] >= ir_ref[...]
            lane = lax.broadcasted_iota(jnp.int32, (rows, LANES), 1)
            all_lse = jnp.zeros((rows, LANES), F32)
            for pair in range(heads_w // LANES):
                at = pair * LANES
                q_raw = acc[:, at : at + LANES]
                k_raw = acc[:, heads_w + at : heads_w + at + LANES]
                q = (q_raw * cos + rotated(q_raw) * sin).astype(BF16)
                k = (k_raw * cos + rotated(k_raw) * sin).astype(BF16)
                v = acc[:, 2 * heads_w + at : 2 * heads_w + at + LANES].astype(BF16)
                qkv_ref[:, at : at + LANES] = q
                qkv_ref[:, heads_w + at : heads_w + at + LANES] = k
                qkv_ref[:, 2 * heads_w + at : 2 * heads_w + at + LANES] = v
                mixed = None
                for half in range(2):
                    mine = (lane // HD) == half
                    scores = mm(jnp.where(mine, q, jnp.zeros_like(q)), k, NT) * SCALE
                    scores = jnp.where(seen, scores, -jnp.inf)
                    top = jnp.max(scores, axis=-1, keepdims=True)
                    raised = jnp.exp(scores - top)
                    total = jnp.sum(raised, axis=-1, keepdims=True)
                    all_lse = jnp.where(lane == 2 * pair + half, top + jnp.log(total), all_lse)
                    probs = (raised * (1.0 / total)).astype(BF16)
                    term = mm(probs, jnp.where(mine, v, jnp.zeros_like(v)))
                    mixed = term if mixed is None else mixed + term
                o_ref[:, at : at + LANES] = mixed.astype(BF16)
            lse_ref[...] = all_lse

    @pl.when(phase == 1)
    def _():
        part = mm(o_ref[...], wo_ref[0])
        keep_ref[...] = part[: rows // 2]
        send_ref[...] = part[rows // 2 :].astype(BF16)


def attn_fwd(normed, weights, w_out, tables):
    cos, sin, id_col, id_row = tables
    rows, width = normed.shape
    steps, _, three = weights.shape
    heads_w, shard = w_out.shape[1], w_out.shape[2]
    early = lambda p, w: p * (steps - 1) + (1 - p) * w
    late = lambda p, w: p * w
    full = lambda a: pl.BlockSpec(a.shape, lambda p, w: (0, 0))
    return pl.pallas_call(
        functools.partial(attn_fwd_kernel, steps),
        grid=(2, steps),
        in_specs=[
            pl.BlockSpec((rows, shard), lambda p, w: (0, early(p, w))),
            pl.BlockSpec((1, shard, three), lambda p, w: (early(p, w), 0, 0)),
            pl.BlockSpec((1, heads_w, shard), lambda p, w: (late(p, w), 0, 0)),
            full(cos), full(sin), full(id_col), full(id_row),
        ],
        out_specs=[
            pl.BlockSpec((rows, three), lambda p, w: (0, 0)),
            pl.BlockSpec((rows, LANES), lambda p, w: (0, 0)),
            pl.BlockSpec((rows, heads_w), lambda p, w: (0, 0)),
            pl.BlockSpec((rows // 2, shard), lambda p, w: (0, late(p, w))),
            pl.BlockSpec((rows // 2, shard), lambda p, w: (0, late(p, w))),
        ],
        out_shape=(
            jax.ShapeDtypeStruct((rows, three), BF16),
            jax.ShapeDtypeStruct((rows, LANES), F32),
            jax.ShapeDtypeStruct((rows, heads_w), BF16),
            jax.ShapeDtypeStruct((rows // 2, width), F32),
            jax.ShapeDtypeStruct((rows // 2, width), BF16),
        ),
        scratch_shapes=[pltpu.VMEM((rows, three), F32)],
        cost_estimate=cost(
            2 * rows * width * (three + heads_w) + 8 * rows * rows * heads_w,
            2 * width * (three + heads_w) + 12 * rows * width,
            rows * rows * heads_w // HD,
        ),
        name="attn_fwd",
    )(normed, weights, w_out, cos, sin, id_col, id_row)


def attn_bwd_kernel(
    steps, db_ref, wo_ref, w_ref, qkv_ref, lse_ref, cos_ref, sin_ref, ic_ref, ir_ref,
    dqkv_ref, keep_ref, send_ref, acc,
):
    phase, step = pl.program_id(0), pl.program_id(1)
    rows = db_ref.shape[0]
    heads_w = acc.shape[1]

    @pl.when(phase == 0)
    def _():
        term = mm(db_ref[...], wo_ref[0], NT)

        @pl.when(step == 0)
        def _():
            acc[...] = term

        @pl.when(step > 0)
        def _():
            acc[...] += term

        @pl.when(step == steps - 1)
        def _():
            cos, sin = cos_ref[...], sin_ref[...]
            seen = ic_ref[...] >= ir_ref[...]
            lane = lax.broadcasted_iota(jnp.int32, (rows, LANES), 1)
            all_lse = lse_ref[...]
            for pair in range(heads_w // LANES):
                at = pair * LANES
                q = qkv_ref[:, at : at + LANES]
                k = qkv_ref[:, heads_w + at : heads_w + at + LANES]
                v = qkv_ref[:, 2 * heads_w + at : 2 * heads_w + at + LANES]
                d_o = acc[:, at : at + LANES].astype(BF16)
                grads = [None, None, None]
                for half in range(2):
                    mine = (lane // HD) == half
                    only = lambda a: jnp.where(mine, a, jnp.zeros_like(a))
                    q_m, d_m = only(q), only(d_o)
                    scores = mm(q_m, k, NT) * SCALE
                    index = 2 * pair + half
                    probs = jnp.exp(scores - all_lse[:, index : index + 1])
                    probs = jnp.where(seen, probs, 0.0)
                    d_probs = mm(d_m, v, NT)
                    row_dot = jnp.sum(probs * d_probs, axis=-1, keepdims=True)
                    d_s = (probs * (d_probs - row_dot) * SCALE).astype(BF16)
                    terms = (
                        mm(d_s, only(k)),
                        mm(d_s, q_m, TN),
                        mm(probs.astype(BF16), d_m, TN),
                    )
                    grads = [t if g is None else g + t for g, t in zip(grads, terms)]
                d_q = grads[0] * cos - rotated(grads[0]) * sin
                d_k = grads[1] * cos - rotated(grads[1]) * sin
                dqkv_ref[:, at : at + LANES] = d_q.astype(BF16)
                dqkv_ref[:, heads_w + at : heads_w + at + LANES] = d_k.astype(BF16)
                dqkv_ref[:, 2 * heads_w + at : 2 * heads_w + at + LANES] = grads[2].astype(BF16)

    @pl.when(phase == 1)
    def _():
        part = mm(dqkv_ref[...], w_ref[0], NT)
        keep_ref[...] = part[: rows // 2]
        send_ref[...] = part[rows // 2 :].astype(BF16)


def attn_bwd(d_rows, weights, w_out, qkv, lse, tables):
    cos, sin, id_col, id_row = tables
    rows, width = d_rows.shape
    steps, _, three = weights.shape
    heads_w, shard = w_out.shape[1], w_out.shape[2]
    early = lambda p, w: p * (steps - 1) + (1 - p) * w
    late = lambda p, w: p * w
    full = lambda a: pl.BlockSpec(a.shape, lambda p, w: (0, 0))
    return pl.pallas_call(
        functools.partial(attn_bwd_kernel, steps),
        grid=(2, steps),
        in_specs=[
            pl.BlockSpec((rows, shard), lambda p, w: (0, early(p, w))),
            pl.BlockSpec((1, heads_w, shard), lambda p, w: (early(p, w), 0, 0)),
            pl.BlockSpec((1, shard, three), lambda p, w: (late(p, w), 0, 0)),
            full(qkv), full(lse), full(cos), full(sin), full(id_col), full(id_row),
        ],
        out_specs=[
            pl.BlockSpec((rows, three), lambda p, w: (0, 0)),
            pl.BlockSpec((rows // 2, shard), lambda p, w: (0, late(p, w))),
            pl.BlockSpec((rows // 2, shard), lambda p, w: (0, late(p, w))),
        ],
        out_shape=(
            jax.ShapeDtypeStruct((rows, three), BF16),
            jax.ShapeDtypeStruct((rows // 2, width), F32),
            jax.ShapeDtypeStruct((rows // 2, width), BF16),
        ),
        scratch_shapes=[pltpu.VMEM((rows, heads_w), F32)],
        cost_estimate=cost(
            2 * rows * width * (three + heads_w) + 20 * rows * rows * heads_w,
            2 * width * (three + heads_w) + 14 * rows * width,
            rows * rows * heads_w // HD,
        ),
        name="attn_bwd",
    )(d_rows, w_out, weights, qkv, lse, cos, sin, id_col, id_row)


def mlp_fwd_kernel(
    steps, n_ref, wg_ref, wu_ref, wd_ref, gate_ref, up_ref, keep_ref, send_ref, acc
):
    step = pl.program_id(0)
    rows = n_ref.shape[0]
    normed = n_ref[...]
    gate = mm(normed, wg_ref[...])
    up = mm(normed, wu_ref[...])
    gate_ref[...] = gate
    up_ref[...] = up
    hid = (gate * jax.nn.sigmoid(gate) * up).astype(BF16)
    shard = wd_ref.shape[2]
    for piece in range(wd_ref.shape[0]):
        at = piece * shard
        term = mm(hid, wd_ref[piece])

        @pl.when(step == 0)
        def _():
            acc[:, at : at + shard] = term

        @pl.when(step > 0)
        def _():
            acc[:, at : at + shard] += term

    @pl.when(step == steps - 1)
    def _():
        keep_ref[...] = acc[: rows // 2]
        send_ref[...] = acc[rows // 2 :].astype(BF16)


def mlp_fwd(normed, w_gate, w_up, w_down):
    rows, width = normed.shape
    units = w_gate.shape[1]
    pieces, _, shard = w_down.shape
    block = min(512, units)
    steps = units // block
    return pl.pallas_call(
        functools.partial(mlp_fwd_kernel, steps),
        grid=(steps,),
        in_specs=[
            pl.BlockSpec((rows, width), lambda f: (0, 0)),
            pl.BlockSpec((width, block), lambda f: (0, f)),
            pl.BlockSpec((width, block), lambda f: (0, f)),
            pl.BlockSpec((pieces, block, shard), lambda f: (0, f, 0)),
        ],
        out_specs=[
            pl.BlockSpec((rows, block), lambda f: (0, f)),
            pl.BlockSpec((rows, block), lambda f: (0, f)),
            pl.BlockSpec((rows // 2, width), lambda f: (0, 0)),
            pl.BlockSpec((rows // 2, width), lambda f: (0, 0)),
        ],
        out_shape=(
            jax.ShapeDtypeStruct((rows, units), F32),
            jax.ShapeDtypeStruct((rows, units), F32),
            jax.ShapeDtypeStruct((rows // 2, width), F32),
            jax.ShapeDtypeStruct((rows // 2, width), BF16),
        ),
        scratch_shapes=[pltpu.VMEM((rows, width), F32)],
        cost_estimate=cost(
            6 * rows * width * units, 6 * width * units + 8 * rows * units, rows * units
        ),
        name="mlp_fwd",
    )(normed, w_gate, w_up, w_down)


def mlp_bwd_kernel(
    steps, c_ref, wg_ref, wu_ref, wd_ref, gate_ref, up_ref, keep_ref, send_ref, acc
):
    step = pl.program_id(0)
    rows = c_ref.shape[0]
    shard = wd_ref.shape[2]
    d_hid = None
    for piece in range(wd_ref.shape[0]):
        at = piece * shard
        term = mm(c_ref[:, at : at + shard], wd_ref[piece], NT)
        d_hid = term if d_hid is None else d_hid + term
    gate, up = gate_ref[...], up_ref[...]
    sig = jax.nn.sigmoid(gate)
    d_gate = (d_hid * up * sig * (1.0 + gate * (1.0 - sig))).astype(BF16)
    d_up = (d_hid * gate * sig).astype(BF16)
    term = mm(d_gate, wg_ref[...], NT) + mm(d_up, wu_ref[...], NT)

    @pl.when(step == 0)
    def _():
        acc[...] = term

    @pl.when(step > 0)
    def _():
        acc[...] += term

    @pl.when(step == steps - 1)
    def _():
        keep_ref[...] = acc[: rows // 2]
        send_ref[...] = acc[rows // 2 :].astype(BF16)


def mlp_bwd(c_rows, w_gate, w_up, w_down, gate, up):
    rows, width = c_rows.shape
    units = w_gate.shape[1]
    pieces, _, shard = w_down.shape
    block = min(512, units)
    steps = units // block
    return pl.pallas_call(
        functools.partial(mlp_bwd_kernel, steps),
        grid=(steps,),
        in_specs=[
            pl.BlockSpec((rows, width), lambda f: (0, 0)),
            pl.BlockSpec((width, block), lambda f: (0, f)),
            pl.BlockSpec((width, block), lambda f: (0, f)),
            pl.BlockSpec((pieces, block, shard), lambda f: (0, f, 0)),
            pl.BlockSpec((rows, block), lambda f: (0, f)),
            pl.BlockSpec((rows, block), lambda f: (0, f)),
        ],
        out_specs=[
            pl.BlockSpec((rows // 2, width), lambda f: (0, 0)),
            pl.BlockSpec((rows // 2, width), lambda f: (0, 0)),
        ],
        out_shape=(
            jax.ShapeDtypeStruct((rows // 2, width), F32),
            jax.ShapeDtypeStruct((rows // 2, width), BF16),
        ),
        scratch_shapes=[pltpu.VMEM((rows, width), F32)],
        cost_estimate=cost(
            6 * rows * width * units, 6 * width * units + 8 * rows * units, rows * units
        ),
        name="mlp_bwd",
    )(c_rows, w_gate, w_up, w_down, gate, up)


def layer_forward(terms, params, tables):
    gain1, weights, w_out, gain2, w_gate, w_up, w_down = params
    hidden, normed1 = add_norm(terms, gain1)
    qkv, lse, attn_o, keep, send = attn_fwd(gather_rows(normed1), weights, w_out, tables)
    middle, normed2 = add_norm((hidden, *scatter_rows(keep, send)), gain2)
    gate, up, keep, send = mlp_fwd(gather_rows(normed2), w_gate, w_up, w_down)
    first, second = scatter_rows(keep, send)
    out = middle + first + second.astype(F32)
    return out, (hidden, qkv, lse, middle, gate, up), (normed1, normed2, attn_o)


def layer_backward(cotangent, low, kept, params, tables):
    gain1, weights, w_out, gain2, w_gate, w_up, w_down = params
    hidden, qkv, lse, middle, gate, up = kept
    terms = scatter_rows(*mlp_bwd(gather_rows(low), w_gate, w_up, w_down, gate, up))
    d_mid, mid_low, gain_mlp = norm_back(*terms, middle, gain2, cotangent)
    dqkv, keep, send = attn_bwd(gather_rows(mid_low), weights, w_out, qkv, lse, tables)
    d_in, d_low, gain_attn = norm_back(*scatter_rows(keep, send), hidden, gain1, d_mid)
    return d_in, d_low, (mid_low, dqkv, gain_attn, gain_mlp)


def over_wide(block):
    return lax.all_gather(block, "wide", axis=0, tiled=False)


def spread_tokens(gathered):
    parts, rows, width = gathered.shape
    return gather_rows(gathered.reshape(parts * rows, width))


def own_columns(gathered, shard):
    start = lax.axis_index("wide") * shard
    return lax.dynamic_slice_in_dim(gathered, start, shard, axis=gathered.ndim - 1)


def wide_major(tokens, parts):
    total, width = tokens.shape
    ranks = lax.axis_size("tensor")
    split = tokens.reshape(ranks, parts, total // (ranks * parts), width)
    return split.transpose(1, 0, 2, 3).reshape(total, width)


def mlp_grads(n2_all, c_all, params, shard):
    w_gate, w_up, w_down = params[4:]
    pieces = w_down.shape[0]

    def chunk_grads(n2, low):
        gate = mm(n2, w_gate)
        up = mm(n2, w_up)
        sig = jax.nn.sigmoid(gate)
        d_hid = sum(
            mm(low[:, i * shard : (i + 1) * shard], w_down[i], NT) for i in range(pieces)
        )
        hid = (gate * sig * up).astype(BF16)
        d_gate = (d_hid * up * sig * (1.0 + gate * (1.0 - sig))).astype(BF16)
        d_up = (d_hid * gate * sig).astype(BF16)
        n2_own = own_columns(n2, shard)
        c_own = own_columns(low, shard)
        return mm(n2_own, d_gate, TN), mm(n2_own, d_up, TN), mm(hid, c_own, TN)

    tokens, width = n2_all.shape
    if tokens <= CHUNK:
        return chunk_grads(n2_all, c_all)
    count = tokens // CHUNK
    rows_of = lambda a: a.reshape(count, CHUNK, width)

    def step(sums, rows):
        return tuple(a + b for a, b in zip(sums, chunk_grads(*rows))), None

    units = w_gate.shape[1]
    zeros = tuple(jnp.zeros(s, F32) for s in ((shard, units), (shard, units), (units, shard)))
    return lax.scan(step, zeros, (rows_of(n2_all), rows_of(c_all)))[0]


def attn_grads(n1_own, dqkv_all, o_all, db_own):
    heads_w = o_all.shape[1]
    pick = lambda i: dqkv_all[:, i * heads_w : (i + 1) * heads_w]
    return tuple(mm(n1_own, pick(i), TN) for i in range(3)) + (mm(o_all, db_own, TN),)


def body(
    boundary, positions, attn_gain, w_query, w_key, w_value, w_out, mlp_gain, w_gate, w_up, w_down
):
    parts = lax.axis_size("wide")
    shard = w_query.shape[1]
    heads_w = w_query.shape[2]
    rank = lax.axis_index("tensor")
    is_first = lax.axis_index("section") == 0
    pick = lambda a, b: jnp.where(is_first, a, b)

    gains = jnp.concatenate([attn_gain[0], mlp_gain[0]])
    gains = jnp.pad(gains, (0, 3 * heads_w - gains.shape[0]))
    gains = jnp.broadcast_to(gains[None], (16, 3 * heads_w))
    packed = jnp.concatenate([w_query[0], w_key[0], w_value[0]], axis=1)
    weights = over_wide(jnp.concatenate([packed, gains], axis=0))
    gain_rows = weights[:, shard].astype(F32)
    gain1 = gain_rows[:, :shard].reshape(1, -1)
    gain2 = gain_rows[:, shard : 2 * shard].reshape(1, -1)
    params = (
        gain1,
        weights,
        over_wide(w_out[0]),
        gain2,
        lax.all_gather(w_gate[0], "wide", axis=0, tiled=True),
        lax.all_gather(w_up[0], "wide", axis=0, tiled=True),
        over_wide(w_down[0]),
    )

    ranks = lax.axis_size("tensor")
    order = jnp.array([0, 2, 1, 3]) ^ rank
    reorder = lambda row: row.reshape(ranks, -1)[order].reshape(-1)
    ids = reorder(jnp.arange(LEN, dtype=jnp.int32))

    def tables_of(position_row):
        half = HD // 2
        exponent = 2.0 * jnp.arange(half).astype(F32) / HD
        frequency = jnp.power(jnp.float32(rope_base), -exponent)
        angles = reorder(position_row).astype(F32)[:, None] * frequency[None, :]
        angles = jnp.concatenate([angles] * (LANES // half), axis=-1)
        return (jnp.cos(angles), jnp.sin(angles), ids[:, None], ids[None, :])

    own = boundary[0]
    tables_a = tables_of(pick(positions[0], positions[1]))
    tables_b = tables_of(pick(positions[1], positions[0]))

    forth = lambda x: lax.ppermute(x, "section", [(0, 1)])
    back = lambda x: lax.ppermute(x, "section", [(1, 0)])

    out0, _, _ = layer_forward((own[0],), params, tables_a)
    out1, kept1, rows1 = layer_forward((pick(own[1], forth(out0)),), params, tables_b)
    out2, kept2, rows2 = layer_forward((pick(own[0], forth(out1)),), params, tables_a)

    low0 = own[0].astype(BF16)
    d0, s0, g0 = layer_backward(own[0], low0, kept1, params, tables_b)
    got = back(s0)
    c1 = pick(got.astype(F32), own[1])
    low1 = pick(got, own[1].astype(BF16))
    d1, s1, g1 = layer_backward(c1, low1, kept2, params, tables_a)
    low2 = back(s1)
    d2, _, g2 = layer_backward(low2.astype(F32), low2, kept1, params, tables_b)

    def job(rows, low, mid_low, dqkv):
        normed1, normed2, attn_o = rows
        both = over_wide(jnp.concatenate([normed1, normed2], axis=0))
        count = normed1.shape[0]
        n1_own = own_columns(both[:, :count], shard)
        n1_own = wide_major(spread_tokens(n1_own), parts)
        n2_all = spread_tokens(both[:, count:])
        o_all = over_wide(attn_o).reshape(-1, heads_w)
        c_all = spread_tokens(over_wide(low))
        db_own = wide_major(spread_tokens(own_columns(over_wide(mid_low), shard)), parts)
        dqkv_all = over_wide(dqkv).reshape(-1, 3 * heads_w)
        return attn_grads(n1_own, dqkv_all, o_all, db_own) + mlp_grads(
            n2_all, c_all, params, shard
        )

    grads2 = job(rows2, low1, g1[0], g1[1])
    grads1 = job(rows1, pick(low2, low0), pick(g2[0], g0[0]), pick(g2[1], g0[1]))
    totals = [a + b for a, b in zip(grads1, grads2)]

    gain_sums = jnp.concatenate(
        [g1[i] + pick(g2[i], g0[i]) for i in (2, 3)], axis=0
    )
    gain_sums = own_columns(lax.psum(gain_sums, ("wide", "tensor")), shard)

    ends = pick(jnp.stack([d1, d2]), jnp.stack([out1, out2]))
    grad_q, grad_k, grad_v, grad_o, grad_g, grad_u, grad_d = totals
    return (
        ends[None],
        gain_sums[0][None],
        grad_q[None],
        grad_k[None],
        grad_v[None],
        grad_o[None],
        gain_sums[1][None],
        grad_g[None],
        grad_u[None],
        grad_d[None],
    )


def solution(mesh):
    columns = P("section", "wide", "tensor")
    stripes = P("section", "tensor", "wide")
    row = P("section", "wide")
    tokens = P("section", None, ("wide", "tensor"), None)
    return jax.shard_map(
        body,
        mesh=mesh,
        in_specs=(
            tokens, P(None, "wide"), row, columns, columns, columns, stripes,
            row, columns, columns, stripes,
        ),
        out_specs=(
            tokens, row, columns, columns, columns, stripes, row, columns, columns, stripes,
        ),
        check_vma=False,
    )
```
